32 devices in a mesh: ctx: 16 (over z, y, x), section: 2 (over core).
Axes of the slice: x: 2, y: 2, z: 4, core: 2. Of those that a mesh axis runs over, the one named last changes fastest.
Arguments:
- layer_inputs: bfloat16 [2, 4096, 1536], P('section', 'ctx'), may hold values from -6 to 6
- conv_weight: bfloat16 [2, 3, 1536, 768], P('section', None, 'ctx'), may hold values from -0.09375 to 0.09375
- mix_weight: bfloat16 [2, 768, 1536], P('section', 'ctx'), may hold values from -0.21875 to 0.21875
- bn_scale: float32 [2, 1536], P('section'), may hold values from 0.5 to 2
- bn_shift: float32 [2, 1536], P('section'), may hold values from -4 to 4
- cotangent: bfloat16 [4096, 1536], P('ctx'), may hold values from -6 to 6
Outputs:
- input_grads: bfloat16 [2, 4096, 1536], P('section', 'ctx')
The draws below stay inside these ranges and needn't reach their ends.
All inputs are finite; a program needn't handle non-finite values.
Results may differ from the reference program's by a relative error of at most 0.0053.
Values may be sent and summed in bfloat16 or wider, within the bound.
A program may use at most 64 MiB of HBM per device.

```python
import math
import jax
import jax.numpy as jnp
from jax import lax

C = 1536
H = 768
TAPS = 3
POSITIONS = 4096
LAYERS = 2


def levels(rng, extent, cuts, low, largest):
    def one(dim, blocks):
        draws = jax.random.uniform(jax.random.fold_in(jax.random.fold_in(rng, 6), dim), (blocks,), jnp.float32, low / len(cuts), largest / len(cuts))
        return jnp.repeat(jnp.exp(draws), extent[dim] // blocks).reshape((-1,) + (1,) * (len(extent) - dim - 1))

    loudness = one(*cuts[0])
    for cut in cuts[1:]:
        loudness = loudness * one(*cut)
    return loudness


def noise(key, dims, scale, most, cuts=(), held_as=jnp.bfloat16):
    entries = jax.random.normal(key, dims, jnp.float32) * scale
    if len(cuts) > 0:
        entries = levels(key, dims, cuts, -0.22, 0.18) * entries
    return jnp.clip(entries, min=-most, max=most).astype(held_as)


def setup_inputs(seed: int = 0) -> dict:
    key_list = jax.random.split(jax.random.key(seed), 7)
    layer_inputs = noise(key_list[0], (LAYERS, POSITIONS, C), 1.0, 6.0, ((0, 2), (1, 16)))
    conv_weight = noise(key_list[1], (LAYERS, TAPS, C, H), (3 * C) ** -0.5, 0.09375, ((0, 2), (2, 16)))
    mix_weight = noise(key_list[2], (LAYERS, H, C), H ** -0.5, 0.21875, ((0, 2), (1, 16)))
    bn_scale = jnp.clip(jnp.exp(math.log(2.0) - 1.3862944 * jax.random.uniform(key_list[3], (LAYERS, C), jnp.float32) ** levels(key_list[3], (LAYERS, C), ((0, 2),), -0.2, 0.2)), 0.5, 2.0)
    bn_shift = noise(key_list[4], (LAYERS, C), 1.0, 4.0, ((0, 2),), jnp.float32)
    cotangent = noise(key_list[5], (POSITIONS, C), 1.0, 6.0, ((0, 16),))
    return {"layer_inputs": layer_inputs, "conv_weight": conv_weight, "mix_weight": mix_weight, "bn_scale": bn_scale, "bn_shift": bn_shift, "cotangent": cotangent}


def gelu_parts(value):
    cdf = 0.5 * (1.0 + lax.erf(value * 0.7071067811865476))
    dens = jnp.exp(-0.5 * value * value) * 0.3989422804014327
    return value * cdf, cdf + value * dens


def reference(layer_inputs, conv_weight, mix_weight, bn_scale, bn_shift, cotangent):
    sections = layer_inputs.shape[0]
    total = layer_inputs.shape[1]
    grad = cotangent
    results = [None] * sections
    for level in reversed(range(sections)):
        spacing = 2 ** level
        pre = layer_inputs[level].astype(jnp.float32) * bn_scale[level] + bn_shift[level]
        act, slope_pre = gelu_parts(pre)
        hidden = act.astype(jnp.bfloat16)
        padded = jnp.pad(hidden, ((spacing, spacing), (0, 0)))
        conv = jnp.zeros((total, conv_weight.shape[3]), jnp.float32)
        for k in range(3):
            conv = conv + jnp.dot(padded[k * spacing:k * spacing + total], conv_weight[level, k], preferred_element_type=jnp.float32)
        _, slope_conv = gelu_parts(conv)
        back = jnp.dot(grad, mix_weight[level].T, preferred_element_type=jnp.float32)
        dconv = (back * slope_conv).astype(jnp.bfloat16)
        dpad = jnp.pad(dconv, ((spacing, spacing), (0, 0)))
        dhidden = jnp.zeros((total, conv_weight.shape[2]), jnp.float32)
        for k in range(3):
            begin = (2 - k) * spacing
            dhidden = dhidden + jnp.dot(dpad[begin:begin + total], conv_weight[level, k].T, preferred_element_type=jnp.float32)
        grad = (grad.astype(jnp.float32) + dhidden * slope_pre * bn_scale[level]).astype(jnp.bfloat16)
        results[level] = grad
    return jnp.stack(results)
```

```python
import functools
import jax
import jax.numpy as jnp
from jax import lax
from jax.experimental import pallas as pl
from jax.experimental.pallas import tpu as pltpu
from jax.sharding import PartitionSpec as P

MESH = pl.DeviceIdType.MESH
HOPS = sorted(((t, ry, rx) for t in range(4) for ry in range(2) for rx in range(2)), key=sum)


def place():
    i = lax.axis_index("ctx")
    return i // 4, (i // 2) % 2, i % 2


def at(z, y, x):
    return {"ctx": z * 4 + y * 2 + x}


def greet():
    z, y, x = place()
    barrier = pltpu.get_barrier_semaphore()

    def hello(device):
        pl.semaphore_signal(barrier, inc=1, device_id=device, device_id_type=MESH)

    hello(at(z, y, 1 - x))
    hello(at(z, 1 - y, x))

    @pl.when(z > 0)
    def _():
        hello(at(z - 1, y, x))

    @pl.when(z < 3)
    def _():
        hello(at(z + 1, y, x))

    ends = (z == 0).astype(jnp.int32) + (z == 3).astype(jnp.int32)
    pl.semaphore_wait(barrier, 4 - ends)


class Gather:
    def __init__(self, conv, mix, conv_full, mix_full, send_sem, recv_sem):
        self.conv, self.mix, self.conv_full, self.mix_full = conv, mix, conv_full, mix_full
        self.send_sem, self.recv_sem = send_sem, recv_sem
        depth, inner, wide = conv.shape[2], mix.shape[1], mix.shape[2]
        third = inner // 3
        self.depth, self.inner = depth, inner
        self.parts = (
            ("xzy", (0, 0, depth), (0, 0, wide), third),
            ("yzx", (1, 0, depth), (third, 0, wide), third),
            ("zxy", (2, 0, depth // 2), (2 * third, 0, wide // 2), third),
            ("zyx", (2, depth // 2, depth // 2), (2 * third, wide // 2, wide // 2), third),
        )

    def own(self, part):
        _, (tap, row, rows), (mrow, col, cols), third = self.parts[part]
        return (
            self.conv.at[0, tap, pl.ds(row, rows), :],
            self.mix.at[0, pl.ds(mrow, third), pl.ds(col, cols)],
        )

    def full(self, part, source):
        _, (tap, row, rows), (mrow, col, cols), third = self.parts[part]
        return (
            self.conv_full.at[tap, pl.ds(pl.multiple_of(source * self.depth + row, 16), rows), :],
            self.mix_full.at[pl.ds(pl.multiple_of(source * self.inner + mrow, 16), third), pl.ds(col, cols)],
        )

    def copies(self, part, source, mine, lane, device):
        here = self.own(part) if mine else self.full(part, source)
        there = self.full(part, source)
        return [
            pltpu.make_async_remote_copy(
                src_ref=here[m],
                dst_ref=there[m],
                send_sem=self.send_sem.at[part, source, lane, m],
                recv_sem=self.recv_sem.at[part, source, m],
                device_id=device,
                device_id_type=MESH,
            )
            for m in range(2)
        ]

    def visit(self, t, ry, rx, part, sign, act):
        z, y, x = place()
        source = (z + sign * t) * 4 + (1 - y if ry else y) * 2 + (1 - x if rx else x)
        mine = not (t or ry or rx)
        differs = {"x": rx, "y": ry, "z": t}
        order = self.parts[part][0]
        for n in (2, 1, 0):
            axis = order[n]
            if any(differs[later] for later in order[n + 1:]):
                continue
            if axis == "x" and not rx:
                act(self.copies(part, source, mine, 0, at(z, y, 1 - x)))
            if axis == "y" and not ry:
                act(self.copies(part, source, mine, 1, at(z, 1 - y, x)))
            if axis == "z":
                if t:
                    lane = 2 + (1 + sign) // 2

                    @pl.when((z - sign >= 0) & (z - sign < 4))
                    def _():
                        act(self.copies(part, source, mine, lane, at(z - sign, y, x)))
                else:
                    for lane, step in ((2, 1), (3, -1)):

                        @pl.when((z + step >= 0) & (z + step < 4))
                        def _():
                            act(self.copies(part, source, mine, lane, at(z + step, y, x)))

    def each(self, t, body):
        if t == 0:
            body(0)
        else:
            z = place()[0]

            def side(b, c):
                sign = 1 - 2 * b

                @pl.when((z + sign * t >= 0) & (z + sign * t < 4))
                def _():
                    body(sign)

                return c

            lax.fori_loop(0, 2, side, 0)

    def arrive(self, t, ry, rx, part, sign):
        z, y, x = place()
        source = (z + sign * t) * 4 + (1 - y if ry else y) * 2 + (1 - x if rx else x)
        for copy in self.copies(part, source, False, 0, at(z, y, 1 - x)):
            copy.wait_recv()

    def hop(self, t, ry, rx):
        def body(sign):
            for part in range(4):
                if t or ry or rx:
                    self.arrive(t, ry, rx, part, sign)
                self.visit(t, ry, rx, part, sign, lambda cs: [c.start() for c in cs])

        self.each(t, body)

    def drain(self):
        for t, ry, rx in HOPS:

            def body(sign):
                for part in range(4):
                    self.visit(t, ry, rx, part, sign, lambda cs: [c.wait_send() for c in cs])

            self.each(t, body)


def gather_kernel(conv, mix, conv_full, mix_full, send_sem, recv_sem, own_sem):
    greet()
    gather = Gather(conv, mix, conv_full, mix_full, send_sem, recv_sem)
    gather.hop(0, 0, 0)
    z, y, x = place()
    me = z * 4 + y * 2 + x
    local = [
        pltpu.make_async_copy(
            conv.at[0],
            conv_full.at[:, pl.ds(pl.multiple_of(me * gather.depth, 16), gather.depth), :],
            own_sem.at[0],
        ),
        pltpu.make_async_copy(
            mix.at[0],
            mix_full.at[pl.ds(pl.multiple_of(me * gather.inner, 16), gather.inner), :],
            own_sem.at[1],
        ),
    ]
    for copy in local:
        copy.start()
    for t, ry, rx in HOPS[1:]:
        gather.hop(t, ry, rx)
    for copy in local:
        copy.wait()
    gather.drain()


def gathered(conv, mix):
    count = lax.axis_size("ctx")
    any_space = pl.BlockSpec(memory_space=pl.ANY)
    return pl.pallas_call(
        gather_kernel,
        out_shape=(
            jax.ShapeDtypeStruct((3, count * conv.shape[2], conv.shape[3]), conv.dtype),
            jax.ShapeDtypeStruct((count * mix.shape[1], mix.shape[2]), mix.dtype),
        ),
        in_specs=[any_space] * 2,
        out_specs=(any_space, any_space),
        scratch_shapes=[
            pltpu.SemaphoreType.DMA((4, 16, 4, 2)),
            pltpu.SemaphoreType.DMA((4, 16, 2)),
            pltpu.SemaphoreType.DMA((2,)),
        ],
        compiler_params=pltpu.CompilerParams(collective_id=0, has_side_effects=True),
    )(conv, mix)


def extended(cells, sides, width):
    for axis, dim in sides:
        count = lax.axis_size(axis)
        ends = count - 1
        head = lax.slice_in_dim(cells, 0, width, axis=dim)
        tail = lax.slice_in_dim(cells, cells.shape[dim] - width, cells.shape[dim], axis=dim)
        cells = jnp.concatenate(
            [
                lax.ppermute(tail, axis, [(i, (i + 1) % count) for i in range(ends)]),
                cells,
                lax.ppermute(head, axis, [((i + 1) % count, i) for i in range(ends)]),
            ],
            axis=dim,
        )
    return cells


def shifted(block, axis, distance):
    devices = range(lax.axis_size(axis))
    route = [(i - distance, i) for i in devices if i - distance in devices]
    return lax.ppermute(block, axis, route)


def gelu_parts(value):
    cdf = 0.5 * (1.0 + lax.erf(value * 0.7071067811865476))
    dens = jnp.exp(-0.5 * value * value) * 0.3989422804014327
    return (value * cdf, cdf + value * dens)


def shards(layer_inputs, conv_weight, mix_weight, bn_scale, bn_shift, cotangent):
    sections = lax.axis_size("section")
    level = lax.axis_index("section")
    widest = 2 ** (sections - 1)
    if lax.axis_size("ctx") == 16:
        conv_full, mix_full = gathered(conv_weight, mix_weight)
    else:
        conv_full = lax.all_gather(conv_weight, "ctx", axis=2, tiled=True)[0]
        mix_full = lax.all_gather(mix_weight, "ctx", axis=1, tiled=True)[0]
    rows = cotangent.shape[0]
    inner = mix_full.shape[0]
    spacing = jnp.left_shift(jnp.int32(1), level)
    pre = layer_inputs[0].astype(jnp.float32) * bn_scale[0] + bn_shift[0]
    act, slope_pre = gelu_parts(pre)
    hidden = act.astype(jnp.bfloat16)
    padded = extended(hidden, (("ctx", 0),), widest)
    conv = jnp.zeros((rows, inner), jnp.float32)
    for k in range(3):
        window = lax.dynamic_slice_in_dim(padded, widest + (k - 1) * spacing, rows, 0)
        conv = conv + jnp.dot(window, conv_full[k], preferred_element_type=jnp.float32)
    _, slope_conv = gelu_parts(conv)
    factor = slope_pre * bn_scale[0]

    def make_dconv(grad):
        back = jnp.einsum("pc,hc->ph", grad, mix_full, preferred_element_type=jnp.float32)
        return (back * slope_conv).astype(jnp.bfloat16)

    def skip_dconv(grad):
        return jnp.zeros((rows, inner), jnp.bfloat16)

    def finish(grad, dpad, starts):
        dhidden = jnp.zeros((rows, conv_full.shape[1]), jnp.float32)
        for k in range(3):
            window = lax.dynamic_slice_in_dim(dpad, starts[k], rows, 0)
            dhidden = dhidden + jnp.einsum(
                "ph,ch->pc", window, conv_full[k], preferred_element_type=jnp.float32
            )
        return (grad.astype(jnp.float32) + dhidden * factor).astype(jnp.bfloat16)

    mine = jnp.zeros_like(cotangent)

    def turn(step, carry):
        grad, mine = carry
        active = level == sections - 1 - step
        dconv = lax.cond(active, make_dconv, skip_dconv, grad)
        dpad = extended(dconv, (("ctx", 0),), widest)
        starts = [widest + (1 - k) * spacing for k in range(3)]
        result = lax.cond(active, lambda g: finish(g, dpad, starts), lambda g: g, grad)
        mine = jnp.where(active, result, mine)
        grad = shifted(result, "section", -1)
        return (grad, mine)

    grad, mine = lax.fori_loop(0, sections, turn, (cotangent, mine))
    return mine[None]


def solution(mesh):
    return jax.shard_map(
        shards,
        mesh=mesh,
        in_specs=(
            P("section", "ctx", None),
            P("section", None, "ctx", None),
            P("section", "ctx", None),
            P("section", None),
            P("section", None),
            P("ctx", None),
        ),
        out_specs=P("section", "ctx", None),
        check_vma=False,
    )
```

```python
import jax
import jax.numpy as jnp
from jax import lax
from jax.experimental import pallas as pl
from jax.experimental.pallas import tpu as pltpu
from jax.sharding import PartitionSpec as P

MESH = pl.DeviceIdType.MESH
HOPS = sorted(((t, ry, rx) for t in range(4) for ry in range(2) for rx in range(2)), key=sum)


def place():
    i = lax.axis_index("ctx")
    return i // 4, (i // 2) % 2, i % 2


def at(z, y, x):
    return {"ctx": z * 4 + y * 2 + x}


def greet():
    z, y, x = place()
    i = lax.axis_index("ctx")
    barrier = pltpu.get_barrier_semaphore()

    def hello(device):
        pl.semaphore_signal(barrier, inc=1, device_id=device, device_id_type=MESH)

    hello(at(z, y, 1 - x))
    hello(at(z, 1 - y, x))
    hello({"section": 1 - lax.axis_index("section")})
    for there, device in (
        (z > 0, at(z - 1, y, x)),
        (z < 3, at(z + 1, y, x)),
        (i > 0, {"ctx": i - 1}),
        (i < 15, {"ctx": i + 1}),
    ):

        @pl.when(there)
        def _():
            hello(device)

    ends = sum((c).astype(jnp.int32) for c in (z == 0, z == 3, i == 0, i == 15))
    pl.semaphore_wait(barrier, 7 - ends)


class Gather:
    def __init__(self, conv, mix, conv_full, mix_full, send_sem, recv_sem):
        self.conv, self.mix, self.conv_full, self.mix_full = conv, mix, conv_full, mix_full
        self.send_sem, self.recv_sem = send_sem, recv_sem
        depth, inner, wide = conv.shape[2], mix.shape[1], mix.shape[2]
        third = inner // 3
        self.depth, self.inner = depth, inner
        self.parts = (
            ("xzy", (0, 0, depth), (0, 0, wide), third),
            ("yzx", (1, 0, depth), (third, 0, wide), third),
            ("zxy", (2, 0, depth // 2), (2 * third, 0, wide // 2), third),
            ("zyx", (2, depth // 2, depth // 2), (2 * third, wide // 2, wide // 2), third),
        )

    def own(self, part):
        _, (tap, row, rows), (mrow, col, cols), third = self.parts[part]
        return (
            self.conv.at[0, tap, pl.ds(row, rows), :],
            self.mix.at[0, pl.ds(mrow, third), pl.ds(col, cols)],
        )

    def full(self, part, source):
        _, (tap, row, rows), (mrow, col, cols), third = self.parts[part]
        return (
            self.conv_full.at[tap, pl.ds(pl.multiple_of(source * self.depth + row, 16), rows), :],
            self.mix_full.at[pl.ds(pl.multiple_of(source * self.inner + mrow, 16), third), pl.ds(col, cols)],
        )

    def copies(self, part, source, mine, lane, device):
        here = self.own(part) if mine else self.full(part, source)
        there = self.full(part, source)
        return [
            pltpu.make_async_remote_copy(
                src_ref=here[m],
                dst_ref=there[m],
                send_sem=self.send_sem.at[part, source, lane, m],
                recv_sem=self.recv_sem.at[part, source, m],
                device_id=device,
                device_id_type=MESH,
            )
            for m in range(2)
        ]

    def visit(self, t, ry, rx, part, sign, act):
        z, y, x = place()
        source = (z + sign * t) * 4 + (1 - y if ry else y) * 2 + (1 - x if rx else x)
        mine = not (t or ry or rx)
        differs = {"x": rx, "y": ry, "z": t}
        order = self.parts[part][0]
        for n in (2, 1, 0):
            axis = order[n]
            if any(differs[later] for later in order[n + 1:]):
                continue
            if axis == "x" and not rx:
                act(self.copies(part, source, mine, 0, at(z, y, 1 - x)))
            if axis == "y" and not ry:
                act(self.copies(part, source, mine, 1, at(z, 1 - y, x)))
            if axis == "z":
                if t:
                    lane = 2 + (1 + sign) // 2

                    @pl.when((z - sign >= 0) & (z - sign < 4))
                    def _():
                        act(self.copies(part, source, mine, lane, at(z - sign, y, x)))
                else:
                    for lane, step in ((2, 1), (3, -1)):

                        @pl.when((z + step >= 0) & (z + step < 4))
                        def _():
                            act(self.copies(part, source, mine, lane, at(z + step, y, x)))

    def each(self, t, body):
        if t == 0:
            body(0)
        else:
            z = place()[0]

            def side(b, c):
                sign = 1 - 2 * b

                @pl.when((z + sign * t >= 0) & (z + sign * t < 4))
                def _():
                    body(sign)

                return c

            lax.fori_loop(0, 2, side, 0)

    def arrive(self, t, ry, rx, part, sign):
        z, y, x = place()
        source = (z + sign * t) * 4 + (1 - y if ry else y) * 2 + (1 - x if rx else x)
        for copy in self.copies(part, source, False, 0, at(z, y, 1 - x)):
            copy.wait_recv()

    def hop(self, t, ry, rx):
        def body(sign):
            for part in range(4):
                if t or ry or rx:
                    self.arrive(t, ry, rx, part, sign)
                self.visit(t, ry, rx, part, sign, lambda cs: [c.start() for c in cs])

        self.each(t, body)

    def drain(self):
        for t, ry, rx in HOPS:

            def body(sign):
                for part in range(4):
                    self.visit(t, ry, rx, part, sign, lambda cs: [c.wait_send() for c in cs])

            self.each(t, body)


PAD = 16
LANES = 128
TILE = 256


class Halo:
    def __init__(self, middle, halo, send_sem, recv_sem):
        self.middle, self.halo = middle, halo
        self.send_sem, self.recv_sem = send_sem, recv_sem
        self.i = lax.axis_index("ctx")
        self.rows = middle.shape[0]

    def copy(self, slot):
        first = self.rows - PAD if slot == 0 else 0
        return pltpu.make_async_remote_copy(
            src_ref=self.middle.at[pl.ds(first, PAD), :],
            dst_ref=self.halo.at[slot],
            send_sem=self.send_sem.at[slot],
            recv_sem=self.recv_sem.at[slot],
            device_id={"ctx": self.i + 1 if slot == 0 else self.i - 1},
            device_id_type=MESH,
        )

    def sends(self, slot):
        return self.i < 15 if slot == 0 else self.i > 0

    def receives(self, slot):
        return self.i > 0 if slot == 0 else self.i < 15

    def start(self):
        for slot in range(2):

            @pl.when(self.sends(slot))
            def _():
                self.copy(slot).start()

    def finish(self):
        for slot in range(2):

            @pl.when(self.receives(slot))
            def _():
                self.copy(slot).wait_recv()

            @pl.when(jnp.logical_not(self.receives(slot)))
            def _():
                self.halo[slot] = jnp.zeros(self.halo.shape[1:], self.halo.dtype)

            @pl.when(self.sends(slot))
            def _():
                self.copy(slot).wait_send()


def columns(count, width, body):
    def step(n, c):
        body(pl.ds(pl.multiple_of(n * width, width), width), n)
        return c

    lax.fori_loop(0, count, step, 0)


def windows(padded, halo, before, after, level):
    rows, wide = before.shape

    def body(cols, _):
        padded[0:PAD, cols] = halo[0, :, cols].astype(jnp.float32)
        padded[PAD + rows:2 * PAD + rows, cols] = halo[1, :, cols].astype(jnp.float32)
        near = padded[PAD - 1:PAD - 1 + rows, cols]
        far = padded[PAD - 2:PAD - 2 + rows, cols]
        before[:, cols] = jnp.where(level == 0, near, far).astype(jnp.bfloat16)
        near = padded[PAD + 1:PAD + 1 + rows, cols]
        far = padded[PAD + 2:PAD + 2 + rows, cols]
        after[:, cols] = jnp.where(level == 0, near, far).astype(jnp.bfloat16)

    columns(wide // LANES, LANES, body)


def across(left, right):
    return lax.dot_general(left, right, (((1,), (1,)), ((), ())), preferred_element_type=jnp.float32)


def tower_kernel(
    conv_w, mix_w, inputs, scale, shift, cotangent, out,
    conv_full, mix_full, padded, factor, low, mid, high, halo, total,
    dpadded, dlow, dmid, dhigh, dhalo, dtotal, grad,
    send_sem, recv_sem, own_sem, halo_send, halo_recv, dhalo_send, dhalo_recv, grad_send, grad_recv,
):
    level = lax.axis_index("section")
    rows, wide = cotangent.shape
    inner = total.shape[1]
    plane = wide // 4
    greet()
    gather = Gather(conv_w, mix_w, conv_full, mix_full, send_sem, recv_sem)
    gather.hop(0, 0, 0)
    z, y, x = place()
    me = z * 4 + y * 2 + x
    local = [
        pltpu.make_async_copy(
            conv_w.at[0],
            conv_full.at[:, pl.ds(pl.multiple_of(me * gather.depth, 16), gather.depth), :],
            own_sem.at[0],
        ),
        pltpu.make_async_copy(
            mix_w.at[0],
            mix_full.at[pl.ds(pl.multiple_of(me * gather.inner, 16), gather.inner), :],
            own_sem.at[1],
        ),
    ]
    for copy in local:
        copy.start()

    def front(cols, _):
        gain = scale[:, cols]
        pre = inputs[0, :, cols].astype(jnp.float32) * gain + shift[:, cols]
        act, slope = gelu_parts(pre)
        hidden = act.astype(jnp.bfloat16)
        mid[:, cols] = hidden
        padded[PAD:PAD + rows, cols] = hidden.astype(jnp.float32)
        factor[:, cols] = slope * gain

    columns(wide // LANES, LANES, front)

    @pl.when(level == 1)
    def _():
        grad[...] = cotangent[...]

    total[...] = jnp.zeros_like(total)
    edges = Halo(mid, halo, halo_send, halo_recv)
    edges.start()
    for copy in local:
        copy.wait()

    def add_plane(t):
        def body(sign):
            off = pl.ds(pl.multiple_of((z + sign * t) * plane, plane), plane)

            def tile(cols, _):
                part = total[:, cols]
                for k, window in enumerate((low, mid, high)):
                    part += jnp.dot(window[:, off], conv_full[k, off, cols], preferred_element_type=jnp.float32)
                total[:, cols] = part

            columns(inner // TILE, TILE, tile)

        gather.each(t, body)

    for n, (t, ry, rx) in enumerate(HOPS[1:]):
        gather.hop(t, ry, rx)
        if n == 1:
            edges.finish()
            windows(padded, halo, low, high, level)
        if ry and rx:
            add_plane(t)

    def slopes(cols, _):
        total[:, cols] = gelu_parts(total[:, cols])[1]

    columns(inner // LANES, LANES, slopes)

    def hand(n):
        cols = pl.ds(n * TILE, TILE)
        return pltpu.make_async_remote_copy(
            src_ref=out.at[0, :, cols],
            dst_ref=grad.at[:, cols],
            send_sem=grad_send.at[n],
            recv_sem=grad_recv.at[n],
            device_id={"section": 0},
            device_id_type=MESH,
        )

    tiles = wide // TILE

    @pl.when(level == 0)
    def _():
        for n in range(tiles):
            hand_in = pltpu.make_async_remote_copy(
                src_ref=out.at[0, :, pl.ds(n * TILE, TILE)],
                dst_ref=grad.at[:, pl.ds(n * TILE, TILE)],
                send_sem=grad_send.at[n],
                recv_sem=grad_recv.at[n],
                device_id={"section": 1},
                device_id_type=MESH,
            )
            hand_in.wait_recv()

    def back(cols, n):
        value = across(grad[...], mix_full[cols, :]) * total[:, cols]
        dconv = value.astype(jnp.bfloat16)
        dmid[:, cols] = dconv
        dpadded[PAD:PAD + rows, cols] = dconv.astype(jnp.float32)

    columns(inner // TILE, TILE, back)
    dedges = Halo(dmid, dhalo, dhalo_send, dhalo_recv)
    dedges.start()

    def middle(cols, n):
        dtotal[:, cols] = across(dmid[...], conv_full[1, cols, :])

    columns(tiles, TILE, middle)
    dedges.finish()
    windows(dpadded, dhalo, dlow, dhigh, level)
    for n in range(tiles):
        cols = pl.ds(n * TILE, TILE)
        dhidden = dtotal[:, cols] + across(dhigh[...], conv_full[0, cols, :]) + across(dlow[...], conv_full[2, cols, :])
        out[0, :, cols] = (grad[:, cols].astype(jnp.float32) + dhidden * factor[:, cols]).astype(jnp.bfloat16)

        @pl.when(level == 1)
        def _():
            hand(n).start()

    @pl.when(level == 1)
    def _():
        for n in range(tiles):
            hand(n).wait_send()

    gather.drain()


def tower(layer_inputs, conv_weight, mix_weight, bn_scale, bn_shift, cotangent):
    rows, wide = cotangent.shape
    inner = conv_weight.shape[3]
    anywhere = pl.BlockSpec(memory_space=pl.ANY)
    vmem = pl.BlockSpec(memory_space=pltpu.VMEM)
    bf16, f32 = jnp.bfloat16, jnp.float32
    return pl.pallas_call(
        tower_kernel,
        out_shape=jax.ShapeDtypeStruct(layer_inputs.shape, bf16),
        in_specs=[anywhere, anywhere, vmem, vmem, vmem, vmem],
        out_specs=vmem,
        scratch_shapes=[
            pltpu.VMEM((3, wide, inner), bf16),
            pltpu.VMEM((inner, wide), bf16),
            pltpu.VMEM((rows + 2 * PAD, wide), f32),
            pltpu.VMEM((rows, wide), f32),
            pltpu.VMEM((rows, wide), bf16),
            pltpu.VMEM((rows, wide), bf16),
            pltpu.VMEM((rows, wide), bf16),
            pltpu.VMEM((2, PAD, wide), bf16),
            pltpu.VMEM((rows, inner), f32),
            pltpu.VMEM((rows + 2 * PAD, inner), f32),
            pltpu.VMEM((rows, inner), bf16),
            pltpu.VMEM((rows, inner), bf16),
            pltpu.VMEM((rows, inner), bf16),
            pltpu.VMEM((2, PAD, inner), bf16),
            pltpu.VMEM((rows, wide), f32),
            pltpu.VMEM((rows, wide), bf16),
            pltpu.SemaphoreType.DMA((4, 16, 4, 2)),
            pltpu.SemaphoreType.DMA((4, 16, 2)),
            pltpu.SemaphoreType.DMA((2,)),
            pltpu.SemaphoreType.DMA((2,)),
            pltpu.SemaphoreType.DMA((2,)),
            pltpu.SemaphoreType.DMA((2,)),
            pltpu.SemaphoreType.DMA((2,)),
            pltpu.SemaphoreType.DMA((wide // TILE,)),
            pltpu.SemaphoreType.DMA((wide // TILE,)),
        ],
        compiler_params=pltpu.CompilerParams(collective_id=0, has_side_effects=True),
    )(conv_weight, mix_weight, layer_inputs, bn_scale, bn_shift, cotangent)


def extended(cells, sides, width):
    for axis, dim in sides:
        count = lax.axis_size(axis)
        ends = count - 1
        head = lax.slice_in_dim(cells, 0, width, axis=dim)
        tail = lax.slice_in_dim(cells, cells.shape[dim] - width, cells.shape[dim], axis=dim)
        cells = jnp.concatenate(
            [
                lax.ppermute(tail, axis, [(i, (i + 1) % count) for i in range(ends)]),
                cells,
                lax.ppermute(head, axis, [((i + 1) % count, i) for i in range(ends)]),
            ],
            axis=dim,
        )
    return cells


def shifted(block, axis, distance):
    devices = range(lax.axis_size(axis))
    route = [(i - distance, i) for i in devices if i - distance in devices]
    return lax.ppermute(block, axis, route)


def gelu_parts(value):
    cdf = 0.5 * (1.0 + lax.erf(value * 0.7071067811865476))
    dens = jnp.exp(-0.5 * value * value) * 0.3989422804014327
    return (value * cdf, cdf + value * dens)


def shards(layer_inputs, conv_weight, mix_weight, bn_scale, bn_shift, cotangent):
    sections = lax.axis_size("section")
    level = lax.axis_index("section")
    widest = 2 ** (sections - 1)
    if lax.axis_size("ctx") == 16 and sections == 2:
        return tower(layer_inputs, conv_weight, mix_weight, bn_scale, bn_shift, cotangent)
    conv_full = lax.all_gather(conv_weight, "ctx", axis=2, tiled=True)[0]
    mix_full = lax.all_gather(mix_weight, "ctx", axis=1, tiled=True)[0]
    rows = cotangent.shape[0]
    inner = mix_full.shape[0]
    spacing = jnp.left_shift(jnp.int32(1), level)
    pre = layer_inputs[0].astype(jnp.float32) * bn_scale[0] + bn_shift[0]
    act, slope_pre = gelu_parts(pre)
    hidden = act.astype(jnp.bfloat16)
    padded = extended(hidden, (("ctx", 0),), widest)
    conv = jnp.zeros((rows, inner), jnp.float32)
    for k in range(3):
        window = lax.dynamic_slice_in_dim(padded, widest + (k - 1) * spacing, rows, 0)
        conv = conv + jnp.dot(window, conv_full[k], preferred_element_type=jnp.float32)
    _, slope_conv = gelu_parts(conv)
    factor = slope_pre * bn_scale[0]

    def make_dconv(grad):
        back = jnp.einsum("pc,hc->ph", grad, mix_full, preferred_element_type=jnp.float32)
        return (back * slope_conv).astype(jnp.bfloat16)

    def skip_dconv(grad):
        return jnp.zeros((rows, inner), jnp.bfloat16)

    def finish(grad, dpad, starts):
        dhidden = jnp.zeros((rows, conv_full.shape[1]), jnp.float32)
        for k in range(3):
            window = lax.dynamic_slice_in_dim(dpad, starts[k], rows, 0)
            dhidden = dhidden + jnp.einsum(
                "ph,ch->pc", window, conv_full[k], preferred_element_type=jnp.float32
            )
        return (grad.astype(jnp.float32) + dhidden * factor).astype(jnp.bfloat16)

    mine = jnp.zeros_like(cotangent)

    def turn(step, carry):
        grad, mine = carry
        active = level == sections - 1 - step
        dconv = lax.cond(active, make_dconv, skip_dconv, grad)
        dpad = extended(dconv, (("ctx", 0),), widest)
        starts = [widest + (1 - k) * spacing for k in range(3)]
        result = lax.cond(active, lambda g: finish(g, dpad, starts), lambda g: g, grad)
        mine = jnp.where(active, result, mine)
        grad = shifted(result, "section", -1)
        return (grad, mine)

    grad, mine = lax.fori_loop(0, sections, turn, (cotangent, mine))
    return mine[None]


def solution(mesh):
    return jax.shard_map(
        shards,
        mesh=mesh,
        in_specs=(
            P("section", "ctx", None),
            P("section", None, "ctx", None),
            P("section", "ctx", None),
            P("section", None),
            P("section", None),
            P("ctx", None),
        ),
        out_specs=P("section", "ctx", None),
        check_vma=False,
    )
```

```python
import jax
import jax.numpy as jnp
from jax import lax
from jax.experimental import pallas as pl
from jax.experimental.pallas import tpu as pltpu
from jax.sharding import PartitionSpec as P

MESH = pl.DeviceIdType.MESH
HOPS = sorted(((t, ry, rx) for t in range(4) for ry in range(2) for rx in range(2)), key=sum)


def place():
    i = lax.axis_index("ctx")
    return i // 4, (i // 2) % 2, i % 2


def at(z, y, x):
    return {"ctx": z * 4 + y * 2 + x}


def greet():
    z, y, x = place()
    i = lax.axis_index("ctx")
    barrier = pltpu.get_barrier_semaphore()

    def hello(device):
        pl.semaphore_signal(barrier, inc=1, device_id=device, device_id_type=MESH)

    hello(at(z, y, 1 - x))
    hello(at(z, 1 - y, x))
    hello({"section": 1 - lax.axis_index("section")})
    for there, device in (
        (z > 0, at(z - 1, y, x)),
        (z < 3, at(z + 1, y, x)),
        (i > 0, {"ctx": i - 1}),
        (i < 15, {"ctx": i + 1}),
    ):

        @pl.when(there)
        def _():
            hello(device)

    ends = sum((c).astype(jnp.int32) for c in (z == 0, z == 3, i == 0, i == 15))
    pl.semaphore_wait(barrier, 7 - ends)


class Gather:
    def __init__(self, conv, mix, conv_full, mix_full, send_sem, recv_sem):
        self.conv, self.mix, self.conv_full, self.mix_full = conv, mix, conv_full, mix_full
        self.send_sem, self.recv_sem = send_sem, recv_sem
        depth, inner, wide = conv.shape[2], mix.shape[1], mix.shape[2]
        third = inner // 3
        self.depth, self.inner = depth, inner
        self.parts = (
            ("xzy", (0, 0, depth), (0, 0, wide), third),
            ("yzx", (1, 0, depth), (third, 0, wide), third),
            ("zxy", (2, 0, depth // 2), (2 * third, 0, wide // 2), third),
            ("zyx", (2, depth // 2, depth // 2), (2 * third, wide // 2, wide // 2), third),
        )

    def own(self, part):
        _, (tap, row, rows), (mrow, col, cols), third = self.parts[part]
        return (
            self.conv.at[0, tap, pl.ds(row, rows), :],
            self.mix.at[0, pl.ds(mrow, third), pl.ds(col, cols)],
        )

    def full(self, part, source):
        _, (tap, row, rows), (mrow, col, cols), third = self.parts[part]
        return (
            self.conv_full.at[tap, pl.ds(pl.multiple_of(source * self.depth + row, 16), rows), :],
            self.mix_full.at[pl.ds(pl.multiple_of(source * self.inner + mrow, 16), third), pl.ds(col, cols)],
        )

    def copies(self, part, source, mine, lane, device):
        here = self.own(part) if mine else self.full(part, source)
        there = self.full(part, source)
        return [
            pltpu.make_async_remote_copy(
                src_ref=here[m],
                dst_ref=there[m],
                send_sem=self.send_sem.at[part, source, lane, m],
                recv_sem=self.recv_sem.at[part, source, m],
                device_id=device,
                device_id_type=MESH,
            )
            for m in range(2)
        ]

    def visit(self, t, ry, rx, part, sign, act):
        z, y, x = place()
        source = (z + sign * t) * 4 + (1 - y if ry else y) * 2 + (1 - x if rx else x)
        mine = not (t or ry or rx)
        differs = {"x": rx, "y": ry, "z": t}
        order = self.parts[part][0]
        for n in (2, 1, 0):
            axis = order[n]
            if any(differs[later] for later in order[n + 1:]):
                continue
            if axis == "x" and not rx:
                act(self.copies(part, source, mine, 0, at(z, y, 1 - x)))
            if axis == "y" and not ry:
                act(self.copies(part, source, mine, 1, at(z, 1 - y, x)))
            if axis == "z":
                if t:
                    lane = 2 + (1 + sign) // 2

                    @pl.when((z - sign >= 0) & (z - sign < 4))
                    def _():
                        act(self.copies(part, source, mine, lane, at(z - sign, y, x)))
                else:
                    for lane, step in ((2, 1), (3, -1)):

                        @pl.when((z + step >= 0) & (z + step < 4))
                        def _():
                            act(self.copies(part, source, mine, lane, at(z + step, y, x)))

    def each(self, t, body):
        if t == 0:
            body(0)
        else:
            z = place()[0]

            def side(b, c):
                sign = 1 - 2 * b

                @pl.when((z + sign * t >= 0) & (z + sign * t < 4))
                def _():
                    body(sign)

                return c

            lax.fori_loop(0, 2, side, 0)

    def arrive(self, t, ry, rx, part, sign):
        z, y, x = place()
        source = (z + sign * t) * 4 + (1 - y if ry else y) * 2 + (1 - x if rx else x)
        for copy in self.copies(part, source, False, 0, at(z, y, 1 - x)):
            copy.wait_recv()

    def hop(self, t, ry, rx):
        def body(sign):
            for part in range(4):
                if t or ry or rx:
                    self.arrive(t, ry, rx, part, sign)
                self.visit(t, ry, rx, part, sign, lambda cs: [c.start() for c in cs])

        self.each(t, body)

    def drain(self):
        for t, ry, rx in HOPS:

            def body(sign):
                for part in range(4):
                    self.visit(t, ry, rx, part, sign, lambda cs: [c.wait_send() for c in cs])

            self.each(t, body)


PAD = 16
LANES = 128
TILE = 256
LEAD = 5


class Halo:
    def __init__(self, middle, halo, send_sem, recv_sem):
        self.middle, self.halo = middle, halo
        self.send_sem, self.recv_sem = send_sem, recv_sem
        self.i = lax.axis_index("ctx")
        self.rows = middle.shape[0]

    def copy(self, slot):
        first = self.rows - PAD if slot == 0 else 0
        return pltpu.make_async_remote_copy(
            src_ref=self.middle.at[pl.ds(first, PAD), :],
            dst_ref=self.halo.at[slot],
            send_sem=self.send_sem.at[slot],
            recv_sem=self.recv_sem.at[slot],
            device_id={"ctx": self.i + 1 if slot == 0 else self.i - 1},
            device_id_type=MESH,
        )

    def sends(self, slot):
        return self.i < 15 if slot == 0 else self.i > 0

    def receives(self, slot):
        return self.i > 0 if slot == 0 else self.i < 15

    def start(self):
        for slot in range(2):

            @pl.when(self.sends(slot))
            def _():
                self.copy(slot).start()

    def finish(self):
        for slot in range(2):

            @pl.when(self.receives(slot))
            def _():
                self.copy(slot).wait_recv()

            @pl.when(jnp.logical_not(self.receives(slot)))
            def _():
                self.halo[slot] = jnp.zeros(self.halo.shape[1:], self.halo.dtype)

            @pl.when(self.sends(slot))
            def _():
                self.copy(slot).wait_send()


def columns(count, width, body):
    def step(n, c):
        body(pl.ds(pl.multiple_of(n * width, width), width), n)
        return c

    lax.fori_loop(0, count, step, 0)


def windows(padded, halo, before, after, level):
    rows, wide = before.shape

    def body(cols, _):
        padded[0:PAD, cols] = halo[0, :, cols].astype(jnp.float32)
        padded[PAD + rows:2 * PAD + rows, cols] = halo[1, :, cols].astype(jnp.float32)
        near = padded[PAD - 1:PAD - 1 + rows, cols]
        far = padded[PAD - 2:PAD - 2 + rows, cols]
        before[:, cols] = jnp.where(level == 0, near, far).astype(jnp.bfloat16)
        near = padded[PAD + 1:PAD + 1 + rows, cols]
        far = padded[PAD + 2:PAD + 2 + rows, cols]
        after[:, cols] = jnp.where(level == 0, near, far).astype(jnp.bfloat16)

    columns(wide // LANES, LANES, body)


def across(left, right):
    return lax.dot_general(left, right, (((1,), (1,)), ((), ())), preferred_element_type=jnp.float32)


def tower_kernel(
    conv_w, mix_w, inputs, scale, shift, cotangent, out,
    conv_full, mix_full, padded, factor, low, mid, high, halo, total,
    dpadded, dlow, dmid, dhigh, dhalo, dtotal, grad,
    send_sem, recv_sem, own_sem, halo_send, halo_recv, dhalo_send, dhalo_recv, grad_send, grad_recv, gate,
):
    level = lax.axis_index("section")
    rows, wide = cotangent.shape
    inner = total.shape[1]
    plane = wide // 4
    greet()
    gather = Gather(conv_w, mix_w, conv_full, mix_full, send_sem, recv_sem)

    @pl.when(level == 1)
    def _():
        gather.hop(0, 0, 0)

    z, y, x = place()
    me = z * 4 + y * 2 + x
    local = [
        pltpu.make_async_copy(
            conv_w.at[0],
            conv_full.at[:, pl.ds(pl.multiple_of(me * gather.depth, 16), gather.depth), :],
            own_sem.at[0],
        ),
        pltpu.make_async_copy(
            mix_w.at[0],
            mix_full.at[pl.ds(pl.multiple_of(me * gather.inner, 16), gather.inner), :],
            own_sem.at[1],
        ),
    ]
    for copy in local:
        copy.start()

    def front(cols, _):
        gain = scale[:, cols]
        pre = inputs[0, :, cols].astype(jnp.float32) * gain + shift[:, cols]
        act, slope = gelu_parts(pre)
        hidden = act.astype(jnp.bfloat16)
        mid[:, cols] = hidden
        padded[PAD:PAD + rows, cols] = hidden.astype(jnp.float32)
        factor[:, cols] = slope * gain

    columns(wide // LANES, LANES, front)

    @pl.when(level == 1)
    def _():
        grad[...] = cotangent[...]

    total[...] = jnp.zeros_like(total)
    edges = Halo(mid, halo, halo_send, halo_recv)
    edges.start()
    for copy in local:
        copy.wait()

    @pl.when(level == 0)
    def _():
        pl.semaphore_wait(gate, 1)
        gather.hop(0, 0, 0)

    def add_plane(t):
        def body(sign):
            off = pl.ds(pl.multiple_of((z + sign * t) * plane, plane), plane)

            def tile(cols, _):
                part = total[:, cols]
                for k, window in enumerate((low, mid, high)):
                    part += jnp.dot(window[:, off], conv_full[k, off, cols], preferred_element_type=jnp.float32)
                total[:, cols] = part

            columns(inner // TILE, TILE, tile)

        gather.each(t, body)

    for n, (t, ry, rx) in enumerate(HOPS[1:]):
        gather.hop(t, ry, rx)
        if n == LEAD:

            @pl.when(level == 1)
            def _():
                pl.semaphore_signal(gate, inc=1, device_id={"section": 0}, device_id_type=MESH)

        if n == 1:
            edges.finish()
            windows(padded, halo, low, high, level)
        if ry and rx:
            add_plane(t)

    def slopes(cols, _):
        total[:, cols] = gelu_parts(total[:, cols])[1]

    columns(inner // LANES, LANES, slopes)

    def hand(n):
        cols = pl.ds(n * TILE, TILE)
        return pltpu.make_async_remote_copy(
            src_ref=out.at[0, :, cols],
            dst_ref=grad.at[:, cols],
            send_sem=grad_send.at[n],
            recv_sem=grad_recv.at[n],
            device_id={"section": 0},
            device_id_type=MESH,
        )

    tiles = wide // TILE

    @pl.when(level == 0)
    def _():
        for n in range(tiles):
            hand_in = pltpu.make_async_remote_copy(
                src_ref=out.at[0, :, pl.ds(n * TILE, TILE)],
                dst_ref=grad.at[:, pl.ds(n * TILE, TILE)],
                send_sem=grad_send.at[n],
                recv_sem=grad_recv.at[n],
                device_id={"section": 1},
                device_id_type=MESH,
            )
            hand_in.wait_recv()

    def back(cols, n):
        value = across(grad[...], mix_full[cols, :]) * total[:, cols]
        dconv = value.astype(jnp.bfloat16)
        dmid[:, cols] = dconv
        dpadded[PAD:PAD + rows, cols] = dconv.astype(jnp.float32)

    columns(inner // TILE, TILE, back)
    dedges = Halo(dmid, dhalo, dhalo_send, dhalo_recv)
    dedges.start()

    def middle(cols, n):
        dtotal[:, cols] = across(dmid[...], conv_full[1, cols, :])

    columns(tiles, TILE, middle)
    dedges.finish()
    windows(dpadded, dhalo, dlow, dhigh, level)
    for n in range(tiles):
        cols = pl.ds(n * TILE, TILE)
        dhidden = dtotal[:, cols] + across(dhigh[...], conv_full[0, cols, :]) + across(dlow[...], conv_full[2, cols, :])
        out[0, :, cols] = (grad[:, cols].astype(jnp.float32) + dhidden * factor[:, cols]).astype(jnp.bfloat16)

        @pl.when(level == 1)
        def _():
            hand(n).start()

    @pl.when(level == 1)
    def _():
        for n in range(tiles):
            hand(n).wait_send()

    gather.drain()


def tower(layer_inputs, conv_weight, mix_weight, bn_scale, bn_shift, cotangent):
    rows, wide = cotangent.shape
    inner = conv_weight.shape[3]
    anywhere = pl.BlockSpec(memory_space=pl.ANY)
    vmem = pl.BlockSpec(memory_space=pltpu.VMEM)
    bf16, f32 = jnp.bfloat16, jnp.float32
    return pl.pallas_call(
        tower_kernel,
        out_shape=jax.ShapeDtypeStruct(layer_inputs.shape, bf16),
        in_specs=[anywhere, anywhere, vmem, vmem, vmem, vmem],
        out_specs=vmem,
        scratch_shapes=[
            pltpu.VMEM((3, wide, inner), bf16),
            pltpu.VMEM((inner, wide), bf16),
            pltpu.VMEM((rows + 2 * PAD, wide), f32),
            pltpu.VMEM((rows, wide), f32),
            pltpu.VMEM((rows, wide), bf16),
            pltpu.VMEM((rows, wide), bf16),
            pltpu.VMEM((rows, wide), bf16),
            pltpu.VMEM((2, PAD, wide), bf16),
            pltpu.VMEM((rows, inner), f32),
            pltpu.VMEM((rows + 2 * PAD, inner), f32),
            pltpu.VMEM((rows, inner), bf16),
            pltpu.VMEM((rows, inner), bf16),
            pltpu.VMEM((rows, inner), bf16),
            pltpu.VMEM((2, PAD, inner), bf16),
            pltpu.VMEM((rows, wide), f32),
            pltpu.VMEM((rows, wide), bf16),
            pltpu.SemaphoreType.DMA((4, 16, 4, 2)),
            pltpu.SemaphoreType.DMA((4, 16, 2)),
            pltpu.SemaphoreType.DMA((2,)),
            pltpu.SemaphoreType.DMA((2,)),
            pltpu.SemaphoreType.DMA((2,)),
            pltpu.SemaphoreType.DMA((2,)),
            pltpu.SemaphoreType.DMA((2,)),
            pltpu.SemaphoreType.DMA((wide // TILE,)),
            pltpu.SemaphoreType.DMA((wide // TILE,)),
            pltpu.SemaphoreType.REGULAR,
        ],
        compiler_params=pltpu.CompilerParams(collective_id=0, has_side_effects=True),
    )(conv_weight, mix_weight, layer_inputs, bn_scale, bn_shift, cotangent)


def extended(cells, sides, width):
    for axis, dim in sides:
        count = lax.axis_size(axis)
        ends = count - 1
        head = lax.slice_in_dim(cells, 0, width, axis=dim)
        tail = lax.slice_in_dim(cells, cells.shape[dim] - width, cells.shape[dim], axis=dim)
        cells = jnp.concatenate(
            [
                lax.ppermute(tail, axis, [(i, (i + 1) % count) for i in range(ends)]),
                cells,
                lax.ppermute(head, axis, [((i + 1) % count, i) for i in range(ends)]),
            ],
            axis=dim,
        )
    return cells


def shifted(block, axis, distance):
    devices = range(lax.axis_size(axis))
    route = [(i - distance, i) for i in devices if i - distance in devices]
    return lax.ppermute(block, axis, route)


def gelu_parts(value):
    cdf = 0.5 * (1.0 + lax.erf(value * 0.7071067811865476))
    dens = jnp.exp(-0.5 * value * value) * 0.3989422804014327
    return (value * cdf, cdf + value * dens)


def shards(layer_inputs, conv_weight, mix_weight, bn_scale, bn_shift, cotangent):
    sections = lax.axis_size("section")
    level = lax.axis_index("section")
    widest = 2 ** (sections - 1)
    if lax.axis_size("ctx") == 16 and sections == 2:
        return tower(layer_inputs, conv_weight, mix_weight, bn_scale, bn_shift, cotangent)
    conv_full = lax.all_gather(conv_weight, "ctx", axis=2, tiled=True)[0]
    mix_full = lax.all_gather(mix_weight, "ctx", axis=1, tiled=True)[0]
    rows = cotangent.shape[0]
    inner = mix_full.shape[0]
    spacing = jnp.left_shift(jnp.int32(1), level)
    pre = layer_inputs[0].astype(jnp.float32) * bn_scale[0] + bn_shift[0]
    act, slope_pre = gelu_parts(pre)
    hidden = act.astype(jnp.bfloat16)
    padded = extended(hidden, (("ctx", 0),), widest)
    conv = jnp.zeros((rows, inner), jnp.float32)
    for k in range(3):
        window = lax.dynamic_slice_in_dim(padded, widest + (k - 1) * spacing, rows, 0)
        conv = conv + jnp.dot(window, conv_full[k], preferred_element_type=jnp.float32)
    _, slope_conv = gelu_parts(conv)
    factor = slope_pre * bn_scale[0]

    def make_dconv(grad):
        back = jnp.einsum("pc,hc->ph", grad, mix_full, preferred_element_type=jnp.float32)
        return (back * slope_conv).astype(jnp.bfloat16)

    def skip_dconv(grad):
        return jnp.zeros((rows, inner), jnp.bfloat16)

    def finish(grad, dpad, starts):
        dhidden = jnp.zeros((rows, conv_full.shape[1]), jnp.float32)
        for k in range(3):
            window = lax.dynamic_slice_in_dim(dpad, starts[k], rows, 0)
            dhidden = dhidden + jnp.einsum(
                "ph,ch->pc", window, conv_full[k], preferred_element_type=jnp.float32
            )
        return (grad.astype(jnp.float32) + dhidden * factor).astype(jnp.bfloat16)

    mine = jnp.zeros_like(cotangent)

    def turn(step, carry):
        grad, mine = carry
        active = level == sections - 1 - step
        dconv = lax.cond(active, make_dconv, skip_dconv, grad)
        dpad = extended(dconv, (("ctx", 0),), widest)
        starts = [widest + (1 - k) * spacing for k in range(3)]
        result = lax.cond(active, lambda g: finish(g, dpad, starts), lambda g: g, grad)
        mine = jnp.where(active, result, mine)
        grad = shifted(result, "section", -1)
        return (grad, mine)

    grad, mine = lax.fori_loop(0, sections, turn, (cotangent, mine))
    return mine[None]


def solution(mesh):
    return jax.shard_map(
        shards,
        mesh=mesh,
        in_specs=(
            P("section", "ctx", None),
            P("section", None, "ctx", None),
            P("section", "ctx", None),
            P("section", None),
            P("section", None),
            P("ctx", None),
        ),
        out_specs=P("section", "ctx", None),
        check_vma=False,
    )
```

```python
import jax
import jax.numpy as jnp
from jax import lax
from jax.experimental import pallas as pl
from jax.experimental.pallas import tpu as pltpu
from jax.sharding import PartitionSpec as P

MESH = pl.DeviceIdType.MESH
HOPS = sorted(((t, ry, rx) for t in range(4) for ry in range(2) for rx in range(2)), key=sum)


def place():
    i = lax.axis_index("ctx")
    return i // 4, (i // 2) % 2, i % 2


def at(z, y, x):
    return {"ctx": z * 4 + y * 2 + x}


def greet():
    z, y, x = place()
    i = lax.axis_index("ctx")
    barrier = pltpu.get_barrier_semaphore()

    def hello(device):
        pl.semaphore_signal(barrier, inc=1, device_id=device, device_id_type=MESH)

    hello(at(z, y, 1 - x))
    hello(at(z, 1 - y, x))
    hello({"section": 1 - lax.axis_index("section")})
    for there, device in (
        (z > 0, at(z - 1, y, x)),
        (z < 3, at(z + 1, y, x)),
        (i > 0, {"ctx": i - 1}),
        (i < 15, {"ctx": i + 1}),
    ):

        @pl.when(there)
        def _():
            hello(device)

    ends = sum((c).astype(jnp.int32) for c in (z == 0, z == 3, i == 0, i == 15))
    pl.semaphore_wait(barrier, 7 - ends)


class Gather:
    def __init__(self, conv, mix, conv_full, mix_full, send_sem, recv_sem):
        self.conv, self.mix, self.conv_full, self.mix_full = conv, mix, conv_full, mix_full
        self.send_sem, self.recv_sem = send_sem, recv_sem
        depth, inner, wide = conv.shape[2], mix.shape[1], mix.shape[2]
        third = inner // 3
        self.depth, self.inner = depth, inner
        self.parts = (
            ("xzy", (0, 0, depth), (0, 0, wide), third),
            ("yzx", (1, 0, depth), (third, 0, wide), third),
            ("zxy", (2, 0, depth // 2), (2 * third, 0, wide // 2), third),
            ("zyx", (2, depth // 2, depth // 2), (2 * third, wide // 2, wide // 2), third),
        )

    def own(self, part):
        _, (tap, row, rows), (mrow, col, cols), third = self.parts[part]
        return (
            self.conv.at[0, tap, pl.ds(row, rows), :],
            self.mix.at[0, pl.ds(mrow, third), pl.ds(col, cols)],
        )

    def full(self, part, source):
        _, (tap, row, rows), (mrow, col, cols), third = self.parts[part]
        return (
            self.conv_full.at[tap, pl.ds(pl.multiple_of(source * self.depth + row, 16), rows), :],
            self.mix_full.at[pl.ds(pl.multiple_of(source * self.inner + mrow, 16), third), pl.ds(col, cols)],
        )

    def copies(self, part, source, mine, lane, device):
        here = self.own(part) if mine else self.full(part, source)
        there = self.full(part, source)
        return [
            pltpu.make_async_remote_copy(
                src_ref=here[m],
                dst_ref=there[m],
                send_sem=self.send_sem.at[part, source, lane, m],
                recv_sem=self.recv_sem.at[part, source, m],
                device_id=device,
                device_id_type=MESH,
            )
            for m in range(2)
        ]

    def visit(self, t, ry, rx, part, sign, act):
        z, y, x = place()
        source = (z + sign * t) * 4 + (1 - y if ry else y) * 2 + (1 - x if rx else x)
        mine = not (t or ry or rx)
        differs = {"x": rx, "y": ry, "z": t}
        order = self.parts[part][0]
        for n in (2, 1, 0):
            axis = order[n]
            if any(differs[later] for later in order[n + 1:]):
                continue
            if axis == "x" and not rx:
                act(self.copies(part, source, mine, 0, at(z, y, 1 - x)))
            if axis == "y" and not ry:
                act(self.copies(part, source, mine, 1, at(z, 1 - y, x)))
            if axis == "z":
                if t:
                    lane = 2 + (1 + sign) // 2

                    @pl.when((z - sign >= 0) & (z - sign < 4))
                    def _():
                        act(self.copies(part, source, mine, lane, at(z - sign, y, x)))
                else:
                    for lane, step in ((2, 1), (3, -1)):

                        @pl.when((z + step >= 0) & (z + step < 4))
                        def _():
                            act(self.copies(part, source, mine, lane, at(z + step, y, x)))

    def each(self, t, body):
        if t == 0:
            body(0)
        else:
            z = place()[0]

            def side(b, c):
                sign = 1 - 2 * b

                @pl.when((z + sign * t >= 0) & (z + sign * t < 4))
                def _():
                    body(sign)

                return c

            lax.fori_loop(0, 2, side, 0)

    def arrive(self, t, ry, rx, part, sign):
        z, y, x = place()
        source = (z + sign * t) * 4 + (1 - y if ry else y) * 2 + (1 - x if rx else x)
        for copy in self.copies(part, source, False, 0, at(z, y, 1 - x)):
            copy.wait_recv()

    def hop(self, t, ry, rx):
        def body(sign):
            for part in range(4):
                if t or ry or rx:
                    self.arrive(t, ry, rx, part, sign)
                self.visit(t, ry, rx, part, sign, lambda cs: [c.start() for c in cs])

        self.each(t, body)

    def drain(self):
        for t, ry, rx in HOPS:

            def body(sign):
                for part in range(4):
                    self.visit(t, ry, rx, part, sign, lambda cs: [c.wait_send() for c in cs])

            self.each(t, body)


PAD = 16
LANES = 128
TILE = 256
LEAD = 2


class Halo:
    def __init__(self, middle, halo, send_sem, recv_sem):
        self.middle, self.halo = middle, halo
        self.send_sem, self.recv_sem = send_sem, recv_sem
        self.i = lax.axis_index("ctx")
        self.rows = middle.shape[0]

    def copy(self, slot):
        first = self.rows - PAD if slot == 0 else 0
        return pltpu.make_async_remote_copy(
            src_ref=self.middle.at[pl.ds(first, PAD), :],
            dst_ref=self.halo.at[slot],
            send_sem=self.send_sem.at[slot],
            recv_sem=self.recv_sem.at[slot],
            device_id={"ctx": self.i + 1 if slot == 0 else self.i - 1},
            device_id_type=MESH,
        )

    def sends(self, slot):
        return self.i < 15 if slot == 0 else self.i > 0

    def receives(self, slot):
        return self.i > 0 if slot == 0 else self.i < 15

    def start(self):
        for slot in range(2):

            @pl.when(self.sends(slot))
            def _():
                self.copy(slot).start()

    def finish(self):
        for slot in range(2):

            @pl.when(self.receives(slot))
            def _():
                self.copy(slot).wait_recv()

            @pl.when(jnp.logical_not(self.receives(slot)))
            def _():
                self.halo[slot] = jnp.zeros(self.halo.shape[1:], self.halo.dtype)

            @pl.when(self.sends(slot))
            def _():
                self.copy(slot).wait_send()


def columns(count, width, body):
    def step(n, c):
        body(pl.ds(pl.multiple_of(n * width, width), width), n)
        return c

    lax.fori_loop(0, count, step, 0)


def windows(padded, halo, before, after, level):
    rows, wide = before.shape

    def body(cols, _):
        padded[0:PAD, cols] = halo[0, :, cols].astype(jnp.float32)
        padded[PAD + rows:2 * PAD + rows, cols] = halo[1, :, cols].astype(jnp.float32)
        near = padded[PAD - 1:PAD - 1 + rows, cols]
        far = padded[PAD - 2:PAD - 2 + rows, cols]
        before[:, cols] = jnp.where(level == 0, near, far).astype(jnp.bfloat16)
        near = padded[PAD + 1:PAD + 1 + rows, cols]
        far = padded[PAD + 2:PAD + 2 + rows, cols]
        after[:, cols] = jnp.where(level == 0, near, far).astype(jnp.bfloat16)

    columns(wide // LANES, LANES, body)


def across(left, right):
    return lax.dot_general(left, right, (((1,), (1,)), ((), ())), preferred_element_type=jnp.float32)


def tower_kernel(
    conv_w, mix_w, inputs, scale, shift, cotangent, out,
    conv_full, mix_full, padded, factor, low, mid, high, halo, total,
    dpadded, dlow, dmid, dhigh, dhalo, dtotal, grad,
    send_sem, recv_sem, own_sem, halo_send, halo_recv, dhalo_send, dhalo_recv, grad_send, grad_recv, gate,
):
    level = lax.axis_index("section")
    rows, wide = cotangent.shape
    inner = total.shape[1]
    plane = wide // 4
    greet()
    gather = Gather(conv_w, mix_w, conv_full, mix_full, send_sem, recv_sem)

    @pl.when(level == 1)
    def _():
        gather.hop(0, 0, 0)

    z, y, x = place()
    me = z * 4 + y * 2 + x
    local = [
        pltpu.make_async_copy(
            conv_w.at[0],
            conv_full.at[:, pl.ds(pl.multiple_of(me * gather.depth, 16), gather.depth), :],
            own_sem.at[0],
        ),
        pltpu.make_async_copy(
            mix_w.at[0],
            mix_full.at[pl.ds(pl.multiple_of(me * gather.inner, 16), gather.inner), :],
            own_sem.at[1],
        ),
    ]
    for copy in local:
        copy.start()

    def front(cols, _):
        gain = scale[:, cols]
        pre = inputs[0, :, cols].astype(jnp.float32) * gain + shift[:, cols]
        act, slope = gelu_parts(pre)
        hidden = act.astype(jnp.bfloat16)
        mid[:, cols] = hidden
        padded[PAD:PAD + rows, cols] = hidden.astype(jnp.float32)
        factor[:, cols] = slope * gain

    columns(wide // LANES, LANES, front)

    @pl.when(level == 1)
    def _():
        grad[...] = cotangent[...]

    total[...] = jnp.zeros_like(total)
    edges = Halo(mid, halo, halo_send, halo_recv)
    edges.start()
    for copy in local:
        copy.wait()

    @pl.when(level == 0)
    def _():
        pl.semaphore_wait(gate, 1)
        gather.hop(0, 0, 0)

    def add_plane(t):
        def body(sign):
            off = pl.ds(pl.multiple_of((z + sign * t) * plane, plane), plane)

            def tile(cols, _):
                part = total[:, cols]
                for k, window in enumerate((low, mid, high)):
                    part += jnp.dot(window[:, off], conv_full[k, off, cols], preferred_element_type=jnp.float32)
                total[:, cols] = part

            columns(inner // TILE, TILE, tile)

        gather.each(t, body)

    for n, (t, ry, rx) in enumerate(HOPS[1:]):
        gather.hop(t, ry, rx)
        if n == LEAD:

            @pl.when(level == 1)
            def _():
                pl.semaphore_signal(gate, inc=1, device_id={"section": 0}, device_id_type=MESH)

        if n == 1:
            edges.finish()
            windows(padded, halo, low, high, level)
        if ry and rx:
            add_plane(t)

    def slopes(cols, _):
        total[:, cols] = gelu_parts(total[:, cols])[1]

    columns(inner // LANES, LANES, slopes)

    def hand(n):
        cols = pl.ds(n * TILE, TILE)
        return pltpu.make_async_remote_copy(
            src_ref=out.at[0, :, cols],
            dst_ref=grad.at[:, cols],
            send_sem=grad_send.at[n],
            recv_sem=grad_recv.at[n],
            device_id={"section": 0},
            device_id_type=MESH,
        )

    tiles = wide // TILE

    @pl.when(level == 0)
    def _():
        for n in range(tiles):
            hand_in = pltpu.make_async_remote_copy(
                src_ref=out.at[0, :, pl.ds(n * TILE, TILE)],
                dst_ref=grad.at[:, pl.ds(n * TILE, TILE)],
                send_sem=grad_send.at[n],
                recv_sem=grad_recv.at[n],
                device_id={"section": 1},
                device_id_type=MESH,
            )
            hand_in.wait_recv()

    def back(cols, n):
        value = across(grad[...], mix_full[cols, :]) * total[:, cols]
        dconv = value.astype(jnp.bfloat16)
        dmid[:, cols] = dconv
        dpadded[PAD:PAD + rows, cols] = dconv.astype(jnp.float32)

    columns(inner // TILE, TILE, back)
    dedges = Halo(dmid, dhalo, dhalo_send, dhalo_recv)
    dedges.start()

    def middle(cols, n):
        dtotal[:, cols] = across(dmid[...], conv_full[1, cols, :])

    columns(tiles, TILE, middle)
    dedges.finish()
    windows(dpadded, dhalo, dlow, dhigh, level)
    for n in range(tiles):
        cols = pl.ds(n * TILE, TILE)
        dhidden = dtotal[:, cols] + across(dhigh[...], conv_full[0, cols, :]) + across(dlow[...], conv_full[2, cols, :])
        out[0, :, cols] = (grad[:, cols].astype(jnp.float32) + dhidden * factor[:, cols]).astype(jnp.bfloat16)

        @pl.when(level == 1)
        def _():
            hand(n).start()

    @pl.when(level == 1)
    def _():
        for n in range(tiles):
            hand(n).wait_send()

    gather.drain()


def tower(layer_inputs, conv_weight, mix_weight, bn_scale, bn_shift, cotangent):
    rows, wide = cotangent.shape
    inner = conv_weight.shape[3]
    anywhere = pl.BlockSpec(memory_space=pl.ANY)
    vmem = pl.BlockSpec(memory_space=pltpu.VMEM)
    bf16, f32 = jnp.bfloat16, jnp.float32
    return pl.pallas_call(
        tower_kernel,
        out_shape=jax.ShapeDtypeStruct(layer_inputs.shape, bf16),
        in_specs=[anywhere, anywhere, vmem, vmem, vmem, vmem],
        out_specs=vmem,
        scratch_shapes=[
            pltpu.VMEM((3, wide, inner), bf16),
            pltpu.VMEM((inner, wide), bf16),
            pltpu.VMEM((rows + 2 * PAD, wide), f32),
            pltpu.VMEM((rows, wide), f32),
            pltpu.VMEM((rows, wide), bf16),
            pltpu.VMEM((rows, wide), bf16),
            pltpu.VMEM((rows, wide), bf16),
            pltpu.VMEM((2, PAD, wide), bf16),
            pltpu.VMEM((rows, inner), f32),
            pltpu.VMEM((rows + 2 * PAD, inner), f32),
            pltpu.VMEM((rows, inner), bf16),
            pltpu.VMEM((rows, inner), bf16),
            pltpu.VMEM((rows, inner), bf16),
            pltpu.VMEM((2, PAD, inner), bf16),
            pltpu.VMEM((rows, wide), f32),
            pltpu.VMEM((rows, wide), bf16),
            pltpu.SemaphoreType.DMA((4, 16, 4, 2)),
            pltpu.SemaphoreType.DMA((4, 16, 2)),
            pltpu.SemaphoreType.DMA((2,)),
            pltpu.SemaphoreType.DMA((2,)),
            pltpu.SemaphoreType.DMA((2,)),
            pltpu.SemaphoreType.DMA((2,)),
            pltpu.SemaphoreType.DMA((2,)),
            pltpu.SemaphoreType.DMA((wide // TILE,)),
            pltpu.SemaphoreType.DMA((wide // TILE,)),
            pltpu.SemaphoreType.REGULAR,
        ],
        compiler_params=pltpu.CompilerParams(collective_id=0, has_side_effects=True),
    )(conv_weight, mix_weight, layer_inputs, bn_scale, bn_shift, cotangent)


def extended(cells, sides, width):
    for axis, dim in sides:
        count = lax.axis_size(axis)
        ends = count - 1
        head = lax.slice_in_dim(cells, 0, width, axis=dim)
        tail = lax.slice_in_dim(cells, cells.shape[dim] - width, cells.shape[dim], axis=dim)
        cells = jnp.concatenate(
            [
                lax.ppermute(tail, axis, [(i, (i + 1) % count) for i in range(ends)]),
                cells,
                lax.ppermute(head, axis, [((i + 1) % count, i) for i in range(ends)]),
            ],
            axis=dim,
        )
    return cells


def shifted(block, axis, distance):
    devices = range(lax.axis_size(axis))
    route = [(i - distance, i) for i in devices if i - distance in devices]
    return lax.ppermute(block, axis, route)


def gelu_parts(value):
    cdf = 0.5 * (1.0 + lax.erf(value * 0.7071067811865476))
    dens = jnp.exp(-0.5 * value * value) * 0.3989422804014327
    return (value * cdf, cdf + value * dens)


def shards(layer_inputs, conv_weight, mix_weight, bn_scale, bn_shift, cotangent):
    sections = lax.axis_size("section")
    level = lax.axis_index("section")
    widest = 2 ** (sections - 1)
    if lax.axis_size("ctx") == 16 and sections == 2:
        return tower(layer_inputs, conv_weight, mix_weight, bn_scale, bn_shift, cotangent)
    conv_full = lax.all_gather(conv_weight, "ctx", axis=2, tiled=True)[0]
    mix_full = lax.all_gather(mix_weight, "ctx", axis=1, tiled=True)[0]
    rows = cotangent.shape[0]
    inner = mix_full.shape[0]
    spacing = jnp.left_shift(jnp.int32(1), level)
    pre = layer_inputs[0].astype(jnp.float32) * bn_scale[0] + bn_shift[0]
    act, slope_pre = gelu_parts(pre)
    hidden = act.astype(jnp.bfloat16)
    padded = extended(hidden, (("ctx", 0),), widest)
    conv = jnp.zeros((rows, inner), jnp.float32)
    for k in range(3):
        window = lax.dynamic_slice_in_dim(padded, widest + (k - 1) * spacing, rows, 0)
        conv = conv + jnp.dot(window, conv_full[k], preferred_element_type=jnp.float32)
    _, slope_conv = gelu_parts(conv)
    factor = slope_pre * bn_scale[0]

    def make_dconv(grad):
        back = jnp.einsum("pc,hc->ph", grad, mix_full, preferred_element_type=jnp.float32)
        return (back * slope_conv).astype(jnp.bfloat16)

    def skip_dconv(grad):
        return jnp.zeros((rows, inner), jnp.bfloat16)

    def finish(grad, dpad, starts):
        dhidden = jnp.zeros((rows, conv_full.shape[1]), jnp.float32)
        for k in range(3):
            window = lax.dynamic_slice_in_dim(dpad, starts[k], rows, 0)
            dhidden = dhidden + jnp.einsum(
                "ph,ch->pc", window, conv_full[k], preferred_element_type=jnp.float32
            )
        return (grad.astype(jnp.float32) + dhidden * factor).astype(jnp.bfloat16)

    mine = jnp.zeros_like(cotangent)

    def turn(step, carry):
        grad, mine = carry
        active = level == sections - 1 - step
        dconv = lax.cond(active, make_dconv, skip_dconv, grad)
        dpad = extended(dconv, (("ctx", 0),), widest)
        starts = [widest + (1 - k) * spacing for k in range(3)]
        result = lax.cond(active, lambda g: finish(g, dpad, starts), lambda g: g, grad)
        mine = jnp.where(active, result, mine)
        grad = shifted(result, "section", -1)
        return (grad, mine)

    grad, mine = lax.fori_loop(0, sections, turn, (cotangent, mine))
    return mine[None]


def solution(mesh):
    return jax.shard_map(
        shards,
        mesh=mesh,
        in_specs=(
            P("section", "ctx", None),
            P("section", None, "ctx", None),
            P("section", "ctx", None),
            P("section", None),
            P("section", None),
            P("ctx", None),
        ),
        out_specs=P("section", "ctx", None),
        check_vma=False,
    )
```

```python
import jax
import jax.numpy as jnp
from jax import lax
from jax.experimental import pallas as pl
from jax.experimental.pallas import tpu as pltpu
from jax.sharding import PartitionSpec as P

MESH = pl.DeviceIdType.MESH
HOPS = sorted(((t, ry, rx) for t in range(4) for ry in range(2) for rx in range(2)), key=sum)


def place():
    i = lax.axis_index("ctx")
    return i // 4, (i // 2) % 2, i % 2


def at(z, y, x):
    return {"ctx": z * 4 + y * 2 + x}


def greet():
    z, y, x = place()
    i = lax.axis_index("ctx")
    barrier = pltpu.get_barrier_semaphore()

    def hello(device):
        pl.semaphore_signal(barrier, inc=1, device_id=device, device_id_type=MESH)

    hello(at(z, y, 1 - x))
    hello(at(z, 1 - y, x))
    hello({"section": 1 - lax.axis_index("section")})
    for there, device in (
        (z > 0, at(z - 1, y, x)),
        (z < 3, at(z + 1, y, x)),
        (i > 0, {"ctx": i - 1}),
        (i < 15, {"ctx": i + 1}),
    ):

        @pl.when(there)
        def _():
            hello(device)

    ends = sum((c).astype(jnp.int32) for c in (z == 0, z == 3, i == 0, i == 15))
    pl.semaphore_wait(barrier, 7 - ends)


class Gather:
    def __init__(self, conv, mix, conv_full, mix_full, send_sem, recv_sem):
        self.conv, self.mix, self.conv_full, self.mix_full = conv, mix, conv_full, mix_full
        self.send_sem, self.recv_sem = send_sem, recv_sem
        depth, inner, wide = conv.shape[2], mix.shape[1], mix.shape[2]
        third = inner // 3
        self.depth, self.inner = depth, inner
        self.parts = (
            ("xzy", (0, 0, depth), (0, 0, wide), third),
            ("yzx", (1, 0, depth), (third, 0, wide), third),
            ("zxy", (2, 0, depth // 2), (2 * third, 0, wide // 2), third),
            ("zyx", (2, depth // 2, depth // 2), (2 * third, wide // 2, wide // 2), third),
        )

    def own(self, part):
        _, (tap, row, rows), (mrow, col, cols), third = self.parts[part]
        return (
            self.conv.at[0, tap, pl.ds(row, rows), :],
            self.mix.at[0, pl.ds(mrow, third), pl.ds(col, cols)],
        )

    def full(self, part, source):
        _, (tap, row, rows), (mrow, col, cols), third = self.parts[part]
        return (
            self.conv_full.at[tap, pl.ds(pl.multiple_of(source * self.depth + row, 16), rows), :],
            self.mix_full.at[pl.ds(pl.multiple_of(source * self.inner + mrow, 16), third), pl.ds(col, cols)],
        )

    def copies(self, part, source, mine, lane, device):
        here = self.own(part) if mine else self.full(part, source)
        there = self.full(part, source)
        return [
            pltpu.make_async_remote_copy(
                src_ref=here[m],
                dst_ref=there[m],
                send_sem=self.send_sem.at[part, source, lane, m],
                recv_sem=self.recv_sem.at[part, source, m],
                device_id=device,
                device_id_type=MESH,
            )
            for m in range(2)
        ]

    def visit(self, t, ry, rx, part, sign, act, legs=(0, 1, 2)):
        z, y, x = place()
        source = (z + sign * t) * 4 + (1 - y if ry else y) * 2 + (1 - x if rx else x)
        mine = not (t or ry or rx)
        differs = {"x": rx, "y": ry, "z": t}
        order = self.parts[part][0]
        for n in legs:
            axis = order[n]
            if any(differs[later] for later in order[n + 1:]):
                continue
            if axis == "x" and not rx:
                act(self.copies(part, source, mine, 0, at(z, y, 1 - x)))
            if axis == "y" and not ry:
                act(self.copies(part, source, mine, 1, at(z, 1 - y, x)))
            if axis == "z":
                if t:
                    lane = 2 + (1 + sign) // 2

                    @pl.when((z - sign >= 0) & (z - sign < 4))
                    def _():
                        act(self.copies(part, source, mine, lane, at(z - sign, y, x)))
                else:
                    for lane, step in ((2, 1), (3, -1)):

                        @pl.when((z + step >= 0) & (z + step < 4))
                        def _():
                            act(self.copies(part, source, mine, lane, at(z + step, y, x)))

    def each(self, t, body):
        if t == 0:
            body(0)
        else:
            z = place()[0]

            def side(b, c):
                sign = 1 - 2 * b

                @pl.when((z + sign * t >= 0) & (z + sign * t < 4))
                def _():
                    body(sign)

                return c

            lax.fori_loop(0, 2, side, 0)

    def arrive(self, t, ry, rx, part, sign):
        z, y, x = place()
        source = (z + sign * t) * 4 + (1 - y if ry else y) * 2 + (1 - x if rx else x)
        for copy in self.copies(part, source, False, 0, at(z, y, 1 - x)):
            copy.wait_recv()

    def begin(self):
        for leg in range(3):
            for part in range(4):
                self.visit(0, 0, 0, part, 0, lambda cs: [c.start() for c in cs], (leg,))

    def hop(self, t, ry, rx):
        def body(sign):
            for part in range(4):
                self.arrive(t, ry, rx, part, sign)
                self.visit(t, ry, rx, part, sign, lambda cs: [c.start() for c in cs])

        self.each(t, body)

    def drain(self):
        for t, ry, rx in HOPS:

            def body(sign):
                for part in range(4):
                    self.visit(t, ry, rx, part, sign, lambda cs: [c.wait_send() for c in cs])

            self.each(t, body)


PAD = 16
LANES = 128
TILE = 256
LEAD = 2


class Halo:
    def __init__(self, middle, halo, send_sem, recv_sem):
        self.middle, self.halo = middle, halo
        self.send_sem, self.recv_sem = send_sem, recv_sem
        self.i = lax.axis_index("ctx")
        self.rows = middle.shape[0]

    def copy(self, slot):
        first = self.rows - PAD if slot == 0 else 0
        return pltpu.make_async_remote_copy(
            src_ref=self.middle.at[pl.ds(first, PAD), :],
            dst_ref=self.halo.at[slot],
            send_sem=self.send_sem.at[slot],
            recv_sem=self.recv_sem.at[slot],
            device_id={"ctx": self.i + 1 if slot == 0 else self.i - 1},
            device_id_type=MESH,
        )

    def sends(self, slot):
        return self.i < 15 if slot == 0 else self.i > 0

    def receives(self, slot):
        return self.i > 0 if slot == 0 else self.i < 15

    def start(self):
        for slot in range(2):

            @pl.when(self.sends(slot))
            def _():
                self.copy(slot).start()

    def finish(self):
        for slot in range(2):

            @pl.when(self.receives(slot))
            def _():
                self.copy(slot).wait_recv()

            @pl.when(jnp.logical_not(self.receives(slot)))
            def _():
                self.halo[slot] = jnp.zeros(self.halo.shape[1:], self.halo.dtype)

            @pl.when(self.sends(slot))
            def _():
                self.copy(slot).wait_send()


def columns(count, width, body):
    def step(n, c):
        body(pl.ds(pl.multiple_of(n * width, width), width), n)
        return c

    lax.fori_loop(0, count, step, 0)


def windows(padded, halo, before, after, level):
    rows, wide = before.shape

    def body(cols, _):
        padded[0:PAD, cols] = halo[0, :, cols].astype(jnp.float32)
        padded[PAD + rows:2 * PAD + rows, cols] = halo[1, :, cols].astype(jnp.float32)
        near = padded[PAD - 1:PAD - 1 + rows, cols]
        far = padded[PAD - 2:PAD - 2 + rows, cols]
        before[:, cols] = jnp.where(level == 0, near, far).astype(jnp.bfloat16)
        near = padded[PAD + 1:PAD + 1 + rows, cols]
        far = padded[PAD + 2:PAD + 2 + rows, cols]
        after[:, cols] = jnp.where(level == 0, near, far).astype(jnp.bfloat16)

    columns(wide // LANES, LANES, body)


def across(left, right):
    return lax.dot_general(left, right, (((1,), (1,)), ((), ())), preferred_element_type=jnp.float32)


def tower_kernel(
    conv_w, mix_w, inputs, scale, shift, cotangent, out,
    conv_full, mix_full, padded, factor, low, mid, high, halo, total,
    dpadded, dlow, dmid, dhigh, dhalo, dtotal, grad,
    send_sem, recv_sem, own_sem, halo_send, halo_recv, dhalo_send, dhalo_recv, grad_send, grad_recv, gate,
):
    level = lax.axis_index("section")
    rows, wide = cotangent.shape
    inner = total.shape[1]
    plane = wide // 4
    greet()
    gather = Gather(conv_w, mix_w, conv_full, mix_full, send_sem, recv_sem)

    @pl.when(level == 1)
    def _():
        gather.begin()

    z, y, x = place()
    me = z * 4 + y * 2 + x
    local = [
        pltpu.make_async_copy(
            conv_w.at[0],
            conv_full.at[:, pl.ds(pl.multiple_of(me * gather.depth, 16), gather.depth), :],
            own_sem.at[0],
        ),
        pltpu.make_async_copy(
            mix_w.at[0],
            mix_full.at[pl.ds(pl.multiple_of(me * gather.inner, 16), gather.inner), :],
            own_sem.at[1],
        ),
    ]
    for copy in local:
        copy.start()

    def front(cols, _):
        gain = scale[:, cols]
        pre = inputs[0, :, cols].astype(jnp.float32) * gain + shift[:, cols]
        act, slope = gelu_parts(pre)
        hidden = act.astype(jnp.bfloat16)
        mid[:, cols] = hidden
        padded[PAD:PAD + rows, cols] = hidden.astype(jnp.float32)
        factor[:, cols] = slope * gain

    columns(wide // LANES, LANES, front)

    @pl.when(level == 1)
    def _():
        grad[...] = cotangent[...]

    total[...] = jnp.zeros_like(total)
    edges = Halo(mid, halo, halo_send, halo_recv)
    edges.start()
    for copy in local:
        copy.wait()

    @pl.when(level == 0)
    def _():
        pl.semaphore_wait(gate, 1)
        gather.begin()

    def add_plane(t):
        def body(sign):
            off = pl.ds(pl.multiple_of((z + sign * t) * plane, plane), plane)

            def tile(cols, _):
                part = total[:, cols]
                for k, window in enumerate((low, mid, high)):
                    part += jnp.dot(window[:, off], conv_full[k, off, cols], preferred_element_type=jnp.float32)
                total[:, cols] = part

            columns(inner // TILE, TILE, tile)

        gather.each(t, body)

    for n, (t, ry, rx) in enumerate(HOPS[1:]):
        gather.hop(t, ry, rx)
        if n == LEAD:

            @pl.when(level == 1)
            def _():
                pl.semaphore_signal(gate, inc=1, device_id={"section": 0}, device_id_type=MESH)

        if n == 1:
            edges.finish()
            windows(padded, halo, low, high, level)
        if ry and rx:
            add_plane(t)

    def slopes(cols, _):
        total[:, cols] = gelu_parts(total[:, cols])[1]

    columns(inner // LANES, LANES, slopes)

    def hand(n):
        cols = pl.ds(n * TILE, TILE)
        return pltpu.make_async_remote_copy(
            src_ref=out.at[0, :, cols],
            dst_ref=grad.at[:, cols],
            send_sem=grad_send.at[n],
            recv_sem=grad_recv.at[n],
            device_id={"section": 0},
            device_id_type=MESH,
        )

    tiles = wide // TILE

    @pl.when(level == 0)
    def _():
        for n in range(tiles):
            hand_in = pltpu.make_async_remote_copy(
                src_ref=out.at[0, :, pl.ds(n * TILE, TILE)],
                dst_ref=grad.at[:, pl.ds(n * TILE, TILE)],
                send_sem=grad_send.at[n],
                recv_sem=grad_recv.at[n],
                device_id={"section": 1},
                device_id_type=MESH,
            )
            hand_in.wait_recv()

    def back(cols, n):
        value = across(grad[...], mix_full[cols, :]) * total[:, cols]
        dconv = value.astype(jnp.bfloat16)
        dmid[:, cols] = dconv
        dpadded[PAD:PAD + rows, cols] = dconv.astype(jnp.float32)

    columns(inner // TILE, TILE, back)
    dedges = Halo(dmid, dhalo, dhalo_send, dhalo_recv)
    dedges.start()

    def middle(cols, n):
        dtotal[:, cols] = across(dmid[...], conv_full[1, cols, :])

    columns(tiles, TILE, middle)
    dedges.finish()
    windows(dpadded, dhalo, dlow, dhigh, level)
    for n in range(tiles):
        cols = pl.ds(n * TILE, TILE)
        dhidden = dtotal[:, cols] + across(dhigh[...], conv_full[0, cols, :]) + across(dlow[...], conv_full[2, cols, :])
        out[0, :, cols] = (grad[:, cols].astype(jnp.float32) + dhidden * factor[:, cols]).astype(jnp.bfloat16)

        @pl.when(level == 1)
        def _():
            hand(n).start()

    @pl.when(level == 1)
    def _():
        for n in range(tiles):
            hand(n).wait_send()

    gather.drain()


def tower(layer_inputs, conv_weight, mix_weight, bn_scale, bn_shift, cotangent):
    rows, wide = cotangent.shape
    inner = conv_weight.shape[3]
    anywhere = pl.BlockSpec(memory_space=pl.ANY)
    vmem = pl.BlockSpec(memory_space=pltpu.VMEM)
    bf16, f32 = jnp.bfloat16, jnp.float32
    return pl.pallas_call(
        tower_kernel,
        out_shape=jax.ShapeDtypeStruct(layer_inputs.shape, bf16),
        in_specs=[anywhere, anywhere, vmem, vmem, vmem, vmem],
        out_specs=vmem,
        scratch_shapes=[
            pltpu.VMEM((3, wide, inner), bf16),
            pltpu.VMEM((inner, wide), bf16),
            pltpu.VMEM((rows + 2 * PAD, wide), f32),
            pltpu.VMEM((rows, wide), f32),
            pltpu.VMEM((rows, wide), bf16),
            pltpu.VMEM((rows, wide), bf16),
            pltpu.VMEM((rows, wide), bf16),
            pltpu.VMEM((2, PAD, wide), bf16),
            pltpu.VMEM((rows, inner), f32),
            pltpu.VMEM((rows + 2 * PAD, inner), f32),
            pltpu.VMEM((rows, inner), bf16),
            pltpu.VMEM((rows, inner), bf16),
            pltpu.VMEM((rows, inner), bf16),
            pltpu.VMEM((2, PAD, inner), bf16),
            pltpu.VMEM((rows, wide), f32),
            pltpu.VMEM((rows, wide), bf16),
            pltpu.SemaphoreType.DMA((4, 16, 4, 2)),
            pltpu.SemaphoreType.DMA((4, 16, 2)),
            pltpu.SemaphoreType.DMA((2,)),
            pltpu.SemaphoreType.DMA((2,)),
            pltpu.SemaphoreType.DMA((2,)),
            pltpu.SemaphoreType.DMA((2,)),
            pltpu.SemaphoreType.DMA((2,)),
            pltpu.SemaphoreType.DMA((wide // TILE,)),
            pltpu.SemaphoreType.DMA((wide // TILE,)),
            pltpu.SemaphoreType.REGULAR,
        ],
        compiler_params=pltpu.CompilerParams(collective_id=0, has_side_effects=True),
    )(conv_weight, mix_weight, layer_inputs, bn_scale, bn_shift, cotangent)


def extended(cells, sides, width):
    for axis, dim in sides:
        count = lax.axis_size(axis)
        ends = count - 1
        head = lax.slice_in_dim(cells, 0, width, axis=dim)
        tail = lax.slice_in_dim(cells, cells.shape[dim] - width, cells.shape[dim], axis=dim)
        cells = jnp.concatenate(
            [
                lax.ppermute(tail, axis, [(i, (i + 1) % count) for i in range(ends)]),
                cells,
                lax.ppermute(head, axis, [((i + 1) % count, i) for i in range(ends)]),
            ],
            axis=dim,
        )
    return cells


def shifted(block, axis, distance):
    devices = range(lax.axis_size(axis))
    route = [(i - distance, i) for i in devices if i - distance in devices]
    return lax.ppermute(block, axis, route)


def gelu_parts(value):
    cdf = 0.5 * (1.0 + lax.erf(value * 0.7071067811865476))
    dens = jnp.exp(-0.5 * value * value) * 0.3989422804014327
    return (value * cdf, cdf + value * dens)


def shards(layer_inputs, conv_weight, mix_weight, bn_scale, bn_shift, cotangent):
    sections = lax.axis_size("section")
    level = lax.axis_index("section")
    widest = 2 ** (sections - 1)
    if lax.axis_size("ctx") == 16 and sections == 2:
        return tower(layer_inputs, conv_weight, mix_weight, bn_scale, bn_shift, cotangent)
    conv_full = lax.all_gather(conv_weight, "ctx", axis=2, tiled=True)[0]
    mix_full = lax.all_gather(mix_weight, "ctx", axis=1, tiled=True)[0]
    rows = cotangent.shape[0]
    inner = mix_full.shape[0]
    spacing = jnp.left_shift(jnp.int32(1), level)
    pre = layer_inputs[0].astype(jnp.float32) * bn_scale[0] + bn_shift[0]
    act, slope_pre = gelu_parts(pre)
    hidden = act.astype(jnp.bfloat16)
    padded = extended(hidden, (("ctx", 0),), widest)
    conv = jnp.zeros((rows, inner), jnp.float32)
    for k in range(3):
        window = lax.dynamic_slice_in_dim(padded, widest + (k - 1) * spacing, rows, 0)
        conv = conv + jnp.dot(window, conv_full[k], preferred_element_type=jnp.float32)
    _, slope_conv = gelu_parts(conv)
    factor = slope_pre * bn_scale[0]

    def make_dconv(grad):
        back = jnp.einsum("pc,hc->ph", grad, mix_full, preferred_element_type=jnp.float32)
        return (back * slope_conv).astype(jnp.bfloat16)

    def skip_dconv(grad):
        return jnp.zeros((rows, inner), jnp.bfloat16)

    def finish(grad, dpad, starts):
        dhidden = jnp.zeros((rows, conv_full.shape[1]), jnp.float32)
        for k in range(3):
            window = lax.dynamic_slice_in_dim(dpad, starts[k], rows, 0)
            dhidden = dhidden + jnp.einsum(
                "ph,ch->pc", window, conv_full[k], preferred_element_type=jnp.float32
            )
        return (grad.astype(jnp.float32) + dhidden * factor).astype(jnp.bfloat16)

    mine = jnp.zeros_like(cotangent)

    def turn(step, carry):
        grad, mine = carry
        active = level == sections - 1 - step
        dconv = lax.cond(active, make_dconv, skip_dconv, grad)
        dpad = extended(dconv, (("ctx", 0),), widest)
        starts = [widest + (1 - k) * spacing for k in range(3)]
        result = lax.cond(active, lambda g: finish(g, dpad, starts), lambda g: g, grad)
        mine = jnp.where(active, result, mine)
        grad = shifted(result, "section", -1)
        return (grad, mine)

    grad, mine = lax.fori_loop(0, sections, turn, (cotangent, mine))
    return mine[None]


def solution(mesh):
    return jax.shard_map(
        shards,
        mesh=mesh,
        in_specs=(
            P("section", "ctx", None),
            P("section", None, "ctx", None),
            P("section", "ctx", None),
            P("section", None),
            P("section", None),
            P("ctx", None),
        ),
        out_specs=P("section", "ctx", None),
        check_vma=False,
    )
```
